32 devices in a mesh: lat: 8 (over y, x, core), rad: 4 (over z).
Axes of the slice: x: 2, y: 2, z: 4, core: 2. Of those that a mesh axis runs over, the one named last changes fastest.
Arguments:
- adjoint_field: float32 [3, 256, 8192], P(None, 'rad', 'lat'), may hold values from -6 to 6
- lateral_coef: float32 [256, 8192], P('rad', 'lat'), may hold values from 0.05 to 0.25
- radial_inverse: float32 [8, 256, 256], P('lat'), may hold values from -0.375 to 0.375
- traction: float32 [8192, 128], P(('lat', 'rad')), may hold values from -6 to 6
- face_plate: int32 [8192, 1], P(('lat', 'rad')), may hold values from 0 to 7; in each aligned block of 256 rows (0 to 255, 256 to 511, ...) at most 128 rows name the same one
- owned_plate: int32 [8], replicated, may hold values from 0 to 7, each once
Outputs:
- corrected: float32 [3, 256, 8192], P(None, 'rad', 'lat')
- plate_grad: float32 [8, 128], P('lat')
The draws below stay inside these ranges and needn't reach their ends.
Inputs may be any that keep to these rules, and one draw needn't show every extreme that they name: `face_plate`: in each aligned block of 256 face blocks (those of one device) no plate appears more than 128 times, and some plate appears exactly 128 times. `owned_plate`: each plate appears exactly once.
All inputs are finite; a program needn't handle non-finite values.
Results may differ from the reference program's by a relative error of at most 0.000075.
Values sent between devices are 32-bit elements; how exact they have to be, the bound alone decides.
No kernel may reach another device: no remote copies, remote signals or barrier semaphores. Data moves between devices by JAX's collectives and lax.ppermute only.
A program may use at most 64 MiB of HBM per device.

```python
import math
import jax
import jax.numpy as jnp
import numpy as np
from jax import lax

NLEV = 256
COMP = 3
W = 128
COL_DEV = 1024
FB = 256
NCOL = 8192
FACES = 8192
NPLATE = 8
CAP = 128
N_LAT = 8
N_RAD = 4


def block_levels(stream_key, shape, pieces, least, top_value):
    level = 1.0
    for axis_at, blocks in pieces:
        heights = jax.random.uniform(jax.random.fold_in(jax.random.fold_in(stream_key, 6), axis_at), (blocks,), jnp.float32, least / len(pieces), top_value / len(pieces))
        level = level * jnp.repeat(jnp.exp(heights), shape[axis_at] // blocks).reshape((-1,) + (1,) * (len(shape) - 1 - axis_at))
    return level


def routed_block(own_key, own, number, rows, count, top, bound, skew):
    order = jax.random.permutation(own_key, count)
    packed, usual = shares(count, rows * top, bound, skew, True), shares(count, rows * top, bound, skew, False)
    places = jnp.arange(count)

    def named(sizes, turn):
        used = int((sizes > 0).sum())
        fixed = max(1, used // 4)
        passed = fixed + (places - fixed + turn * (used - fixed)) % max(1, count - fixed)
        return jnp.zeros((count,), jnp.int32).at[order[jnp.where(places < fixed, places, passed)]].set(jnp.asarray(sizes, jnp.int32))

    sizes = jnp.where(number % 4 == 0, named(packed, number // 4), named(usual, number - number // 4 - 1))
    mixed = jax.random.permutation(jax.random.fold_in(own, 3), count)
    donor, sink = mixed[0:count // 2 * 2:2], mixed[1:count // 2 * 2:2]
    slack = jnp.minimum(sizes[donor] - 1, bound - sizes[sink]) // 2
    slack = jnp.where((donor == order[0]) | (sink == order[0]) | (sizes[sink] == 0), 0, jnp.maximum(slack, 0))
    passed = jax.random.randint(jax.random.fold_in(own, 4), (count // 2,), 0, 1 << 20) % (slack + 1)
    sizes = sizes.at[donor].add(-passed).at[sink].add(passed)
    members = jnp.searchsorted(jnp.cumsum(sizes), jnp.arange(rows * top), side="right").astype(jnp.int32)
    grid = members.reshape(top, rows).T
    grid = grid[jax.random.permutation(jax.random.fold_in(own, 1), rows)]
    turn = jax.random.randint(jax.random.fold_in(own, 2), (rows, 1), 0, top)
    return jnp.take_along_axis(grid, (jnp.arange(top)[None, :] + turn) % top, axis=1)


def shares(count, total, reach, lean, full):
    loads = [(1 << 20) // math.isqrt(rank ** lean) + 1 for rank in range(1, count + 1)]
    largest = reach if full else min(reach, max(-(-total // count), total * loads[0] // sum(loads)))
    least = 1 if total - largest >= count - 1 else 0
    holding, rest = [largest] + [least] * (count - 1), total - largest - least * (count - 1)
    while rest > 0:
        free = [i for i in range(1, count) if holding[i] < largest] or [i for i in range(1, count) if holding[i] < reach]
        whole, left = sum([loads[i] for i in free]), rest
        for i in free:
            extra = min(reach - holding[i], max(1, left * loads[i] // whole), rest)
            holding[i] = holding[i] + extra
            rest = rest - extra
    return np.array(holding)


def noise(stream_key, shape, deviation, bound, split=(), held_as=jnp.bfloat16):
    values = jax.random.normal(stream_key, shape, jnp.float32) * deviation
    if len(split) > 0:
        values = block_levels(stream_key, shape, split, -0.22, 0.18) * values
    return jnp.clip(values, min=-bound, max=bound).astype(held_as)


def setup_inputs(seed: int = 0) -> dict:
    arg_keys = jax.random.split(jax.random.key(seed), 7)
    adjoint_field = noise(arg_keys[0], (COMP, NLEV, NCOL), 1.0, 6.0, ((1, 4), (2, 8)), jnp.float32)
    lateral_coef = jnp.clip(jnp.exp(math.log(0.25) - 1.609438 * jax.random.uniform(arg_keys[1], (NLEV, NCOL), jnp.float32) ** block_levels(arg_keys[1], (NLEV, NCOL), ((0, 4), (1, 8)), -0.2, 0.2)), 0.05, 0.25)
    radial_inverse = noise(arg_keys[2], (N_LAT, NLEV, NLEV), NLEV ** -0.5, 0.375, ((0, 8),), jnp.float32)
    traction = noise(arg_keys[3], (FACES, W), 1.0, 6.0, ((0, 32),), jnp.float32)
    face_plate_keys = jax.random.split(jax.random.fold_in(arg_keys[4], 1), FACES // FB)
    face_plate_turns = jax.random.permutation(jax.random.fold_in(arg_keys[4], 3), FACES // FB)
    face_plate = jax.vmap(lambda own, number: routed_block(jax.random.fold_in(arg_keys[4], 2), own, number, FB, NPLATE, 1, CAP, 2))(face_plate_keys, face_plate_turns).reshape((FACES, 1))
    owned_plate = jax.random.permutation(arg_keys[5], NPLATE).astype(jnp.int32)
    return dict(adjoint_field=adjoint_field, lateral_coef=lateral_coef, radial_inverse=radial_inverse, traction=traction, face_plate=face_plate, owned_plate=owned_plate)


def reference(adjoint_field, lateral_coef, radial_inverse, traction, face_plate, owned_plate):
    padded = jnp.concatenate([adjoint_field[:, :, -1:], adjoint_field, adjoint_field[:, :, :1]], axis=2)
    second = padded[:, :, 2:] + padded[:, :, :-2] - 2.0 * adjoint_field
    smooth = adjoint_field + lateral_coef[None] * second
    blocks = smooth.reshape(COMP, NLEV, N_LAT, COL_DEV)
    correction = jnp.einsum('pkl,clpn->ckpn', radial_inverse, blocks, precision=lax.Precision.HIGHEST)
    corrected = smooth + correction.reshape(COMP, NLEV, NCOL)
    plate_ids = face_plate[:, 0].astype(jnp.int32)
    per_plate = jax.ops.segment_sum(traction, plate_ids, num_segments=NPLATE)
    plate_grad = per_plate[owned_plate.astype(jnp.int32)] * (1.0 / math.sqrt(FB * N_RAD))
    return (corrected, plate_grad)
```

```python
import math

import jax
import jax.numpy as jnp
from jax import lax
from jax.sharding import PartitionSpec as P


def exchanged(x, axis, groups, stride):
    devices = lax.axis_size(axis)
    blocks = [x]
    for k in range(1, groups):
        sends = [(moved(i, -k, groups, stride), i) for i in range(devices)]
        blocks.append(lax.ppermute(x, axis, sends))
    return blocks


def moved(i, k, groups, stride):
    at = i // stride % groups
    return i + ((at + k) % groups - at) * stride


def handed(parts, axis, groups, stride):
    devices = lax.axis_size(axis)
    total = parts[0]
    for k in range(1, groups):
        sends = [(i, moved(i, k, groups, stride)) for i in range(devices)]
        total = total + lax.ppermute(parts[k], axis, sends)
    return total


def product(matrix, blocks):
    stacked = jnp.concatenate(blocks, axis=1)
    return jnp.einsum("kl,cln->ckn", matrix, stacked, precision=lax.Precision.HIGH)


def body(adjoint_field, lateral_coef, radial_inverse, traction, face_plate, owned_plate):
    n_rad, n_lat = lax.axis_size("rad"), lax.axis_size("lat")
    rad, lat = lax.axis_index("rad"), lax.axis_index("lat")
    levels, cols = adjoint_field.shape[1:]
    near = max(d for d in range(1, n_rad + 1) if n_rad % d == 0 and d * d <= n_rad)
    far = n_rad // near
    x, coef = adjoint_field, lateral_coef
    edge = cols // 8

    def inner(a, b):
        mid = x[:, :, a:b]
        return mid + coef[None, :, a:b] * (x[:, :, a - 1 : b - 1] + x[:, :, a + 1 : b + 1] - 2.0 * mid)

    inverse = radial_inverse[0].reshape(n_rad, levels, n_rad, levels)

    def place(i, k, groups, stride):
        at = i // stride % groups
        return i + (lax.rem(at + k, groups) - at) * stride

    def sub(out, sources):
        rows = lax.dynamic_index_in_dim(inverse, out, 0, keepdims=False)
        return jnp.concatenate([lax.dynamic_index_in_dim(rows, s, 1, keepdims=False) for s in sources], axis=1)

    in_far = [place(rad, k, far, near) for k in range(far)]
    in_near = [place(rad, k, near, 1) for k in range(near)]

    near_b = inner(3 * edge, 7 * edge)
    blocks_b = exchanged(near_b, "rad", near, 1)
    far_a1 = inner(edge, 3 * edge)
    blocks_a1 = exchanged(far_a1, "rad", far, near)

    up = [(i, (i + 1) % n_lat) for i in range(n_lat)]
    down = [(j, i) for i, j in up]
    before = lax.ppermute(x[:, :, cols - 1 :], "lat", up)
    after = lax.ppermute(x[:, :, :1], "lat", down)
    left = jnp.concatenate([before, x[:, :, : edge + 1]], axis=2)
    right = jnp.concatenate([x[:, :, cols - edge - 1 :], after], axis=2)
    wide = jnp.concatenate([right, left], axis=2)
    mid = jnp.concatenate([x[:, :, cols - edge :], x[:, :, :edge]], axis=2)
    c2 = jnp.concatenate([coef[:, cols - edge :], coef[:, :edge]], axis=1)
    prev = jnp.concatenate([right[:, :, :-2], left[:, :, :-2]], axis=2)
    nxt = jnp.concatenate([right[:, :, 2:], left[:, :, 2:]], axis=2)
    far_a2 = mid + c2[None] * (prev + nxt - 2.0 * mid)
    blocks_a2 = exchanged(far_a2, "rad", far, near)

    plate_ids = face_plate[:, 0]
    matches = (plate_ids[:, None] == owned_plate[None, :]).astype(jnp.float32)
    sums = jnp.dot(matches.T, traction, precision=lax.Precision.HIGHEST)
    half = n_lat // 2
    while half >= 1:
        bit = lat // half % 2
        keep = lax.dynamic_slice_in_dim(sums, bit * half, half, 0)
        send = lax.dynamic_slice_in_dim(sums, (1 - bit) * half, half, 0)
        sums = keep + lax.ppermute(send, "lat", [(i, i ^ half) for i in range(n_lat)])
        half //= 2
    step = 1
    while step < n_rad:
        sums = sums + lax.ppermute(sums, "rad", [(i, i ^ step) for i in range(n_rad)])
        step *= 2
    plate_grad = sums * (1.0 / math.sqrt(traction.shape[0] * n_rad))

    parts_b = [product(sub(o, in_near), blocks_b) for o in in_far]
    cor_b = handed(parts_b, "rad", far, near)
    parts_a1 = [product(sub(o, in_far), blocks_a1) for o in in_near]
    cor_a1 = handed(parts_a1, "rad", near, 1)
    parts_a2 = [product(sub(o, in_far), blocks_a2) for o in in_near]
    cor_a2 = handed(parts_a2, "rad", near, 1)
    out_b = near_b + cor_b
    out_a1 = far_a1 + cor_a1
    out_a2 = far_a2 + cor_a2
    corrected = jnp.concatenate([out_a2[:, :, edge:], out_a1, out_b, out_a2[:, :, :edge]], axis=2)
    return (corrected, plate_grad)


def solution(mesh):
    in_specs = (
        P(None, "rad", "lat"),
        P("rad", "lat"),
        P("lat", None, None),
        P(("lat", "rad"), None),
        P(("lat", "rad"), None),
        P(),
    )
    out_specs = (P(None, "rad", "lat"), P("lat", None))
    return jax.shard_map(body, mesh=mesh, in_specs=in_specs, out_specs=out_specs, check_vma=False)
```

```python
import math

import jax
import jax.numpy as jnp
from jax import lax
from jax.experimental import pallas as pl
from jax.experimental.pallas import tpu as pltpu
from jax.sharding import PartitionSpec as P


def moved(i, k, size, stride):
    at = i // stride % size
    return i + ((at + k) % size - at) * stride


def hop(x, axis, k, size, stride):
    return lax.ppermute(x, axis, [(i, moved(i, k, size, stride)) for i in range(lax.axis_size(axis))])


def after(x, *earlier):
    return lax.optimization_barrier((x, *earlier))[0]


def vmem_call(kernel, out_shapes, *args):
    return pl.pallas_call(
        kernel,
        out_shape=[pltpu.VMEM(s, jnp.float32) for s in out_shapes],
        in_specs=[pl.BlockSpec(memory_space=pltpu.VMEM)] * len(args),
        out_specs=[pl.BlockSpec(memory_space=pltpu.VMEM)] * len(out_shapes),
    )(*args)


def smooth_kernel(edge, x_ref, coef_ref, b_ref, a1_ref, a2_ref, first_ref, last_ref):
    comps, _, cols = x_ref.shape
    lane = lax.broadcasted_iota(jnp.int32, x_ref.shape[1:], 1)
    coef = coef_ref[...]
    for c in range(comps):
        x = x_ref[c]
        before = jnp.where(lane == 0, 0.0, pltpu.roll(x, 1, 1))
        behind = jnp.where(lane == cols - 1, 0.0, pltpu.roll(x, cols - 1, 1))
        smooth = x + coef * (before + behind - 2.0 * x)
        b_ref[c] = smooth[:, edge : 5 * edge]
        a1_ref[c] = smooth[:, 5 * edge : 7 * edge]
        a2_ref[c, :, :edge] = smooth[:, :edge]
        a2_ref[c, :, edge:] = smooth[:, 7 * edge :]
        first_ref[c] = x[:, :1]
        last_ref[c] = x[:, cols - 1 :]


def close_kernel(edge, open_ref, before_ref, behind_ref, coef_ref, a2_ref):
    cols = coef_ref.shape[1]
    lane = lax.broadcasted_iota(jnp.int32, (open_ref.shape[1], edge), 1)
    for c in range(open_ref.shape[0]):
        left = jnp.where(lane == 0, before_ref[c] * coef_ref[:, :edge], 0.0)
        right = jnp.where(lane == edge - 1, behind_ref[c] * coef_ref[:, cols - edge :], 0.0)
        a2_ref[c, :, :edge] = open_ref[c, :, :edge] + left
        a2_ref[c, :, edge:] = open_ref[c, :, edge:] + right


def product(matrix, stacked):
    return jnp.einsum("kl,cln->ckn", matrix, stacked, precision=lax.Precision.HIGH)


def body(adjoint_field, lateral_coef, radial_inverse, traction, face_plate, owned_plate):
    n_rad, n_lat = lax.axis_size("rad"), lax.axis_size("lat")
    rad, lat = lax.axis_index("rad"), lax.axis_index("lat")
    comps, levels, cols = adjoint_field.shape
    near = max(d for d in range(1, n_rad + 1) if n_rad % d == 0 and d * d <= n_rad)
    far = n_rad // near
    edge = cols // 8

    inverse = radial_inverse[0].reshape(n_rad, levels, n_rad, levels)

    def place(k, size, stride):
        at = lax.div(rad, stride) % size
        return rad + (lax.rem(at + k, size) - at) * stride

    def sub(out, sources):
        rows = lax.dynamic_index_in_dim(inverse, out, 0, keepdims=False)
        return jnp.concatenate([lax.dynamic_index_in_dim(rows, s, 1, keepdims=False) for s in sources], axis=1)

    in_far = [place(k, far, near) for k in range(far)]
    in_near = [place(k, near, 1) for k in range(near)]

    def gather(x, size, stride):
        return [x] + [hop(x, "rad", -k, size, stride) for k in range(1, size)]

    x, coef = adjoint_field, lateral_coef
    wide, thin = (comps, levels, 2 * edge), (comps, levels, 1)
    shapes = ((comps, levels, 4 * edge), wide, wide, thin, thin)
    b, a1, a2_open, first, last = vmem_call(lambda *refs: smooth_kernel(edge, *refs), shapes, x, coef)
    blocks_b = gather(b, near, 1)
    blocks_a1 = gather(a1, far, near)
    before = hop(last, "lat", 1, n_lat, 1)
    behind = hop(first, "lat", -1, n_lat, 1)
    (a2,) = vmem_call(lambda *refs: close_kernel(edge, *refs), (wide,), a2_open, before, behind, coef)
    blocks_a2 = gather(a2, far, near)

    plate_ids = face_plate[:, 0]
    matches = (plate_ids[:, None] == owned_plate[None, :]).astype(jnp.float32)
    sums = jnp.dot(matches.T, traction, precision=lax.Precision.HIGHEST)
    half, k = n_lat // 2, 0
    while half >= 1:
        bit = lat // half % 2
        keep = lax.dynamic_slice_in_dim(sums, bit * half, half, 0)
        send = lax.dynamic_slice_in_dim(sums, (1 - bit) * half, half, 0)
        sums = keep + hop(send, "lat", 1, 2, half)
        half //= 2
        k += 1
    own = sums
    rest = [hop(own, "rad", k, n_rad, 1) for k in range(1, n_rad)]

    def columns(x, blocks, mine, theirs, stride):
        stacked = jnp.concatenate(blocks, axis=1)
        sent = [product(sub(o, theirs), stacked) for o in mine[1:]]
        back = [hop(p, "rad", k, len(mine), stride) for k, p in enumerate(sent, 1)]
        own = after(x + product(sub(mine[0], theirs), stacked))
        return own, back

    own_b, back_b = columns(b, blocks_b, in_far, in_near, near)
    own_a1, back_a1 = columns(a1, blocks_a1, in_near, in_far, 1)
    own_a2, back_a2 = columns(a2, blocks_a2, in_near, in_far, 1)

    total = own
    for r in rest:
        total = total + r
    plate_grad = total * (1.0 / math.sqrt(traction.shape[0] * n_rad))

    out_a1 = sum(back_a1, own_a1)
    out_b = sum(back_b, own_b)
    out_a2 = sum(back_a2, own_a2)
    corrected = jnp.concatenate([out_a2[:, :, :edge], out_b, out_a1, out_a2[:, :, edge:]], axis=2)
    return (corrected, plate_grad)


def solution(mesh):
    in_specs = (
        P(None, "rad", "lat"),
        P("rad", "lat"),
        P("lat", None, None),
        P(("lat", "rad"), None),
        P(("lat", "rad"), None),
        P(),
    )
    out_specs = (P(None, "rad", "lat"), P("lat", None))
    return jax.shard_map(body, mesh=mesh, in_specs=in_specs, out_specs=out_specs, check_vma=False)
```

```python
import math

import jax
import jax.numpy as jnp
from jax import lax
from jax.experimental import pallas as pl
from jax.experimental.pallas import tpu as pltpu
from jax.sharding import PartitionSpec as P

VMEM_BYTES = 8 << 20


def moved(i, k, size, stride):
    at = i // stride % size
    return i + ((at + k) % size - at) * stride


def on_chip(x):
    return pltpu.with_memory_space_constraint(x, pltpu.VMEM)


def vmem_call(kernel, out_shapes, *args, space=pltpu.VMEM, limit=VMEM_BYTES):
    return pl.pallas_call(
        kernel,
        out_shape=[space(s, jnp.float32) for s in out_shapes],
        in_specs=[pl.BlockSpec(memory_space=pltpu.VMEM)] * len(args),
        out_specs=[pl.BlockSpec(memory_space=pltpu.VMEM)] * len(out_shapes),
        compiler_params=pltpu.CompilerParams(vmem_limit_bytes=limit),
    )(*args)


def smooth_kernel(edge, x_ref, coef_ref, a1_ref, b1_ref, b2_ref, a2_ref, first_ref, last_ref):
    comps, _, cols = x_ref.shape
    lane = lax.broadcasted_iota(jnp.int32, x_ref.shape[1:], 1)
    coef = coef_ref[...]
    for c in range(comps):
        x = x_ref[c]
        before = jnp.where(lane == 0, 0.0, pltpu.roll(x, 1, 1))
        behind = jnp.where(lane == cols - 1, 0.0, pltpu.roll(x, cols - 1, 1))
        smooth = x + coef * (before + behind - 2.0 * x)
        a1_ref[c] = smooth[:, edge : 3 * edge]
        b1_ref[c] = smooth[:, 3 * edge : 5 * edge]
        b2_ref[c] = smooth[:, 5 * edge : 7 * edge]
        a2_ref[c, :, :edge] = smooth[:, :edge]
        a2_ref[c, :, edge:] = smooth[:, 7 * edge :]
        first_ref[c] = x[:, :1]
        last_ref[c] = x[:, cols - 1 :]


def close_kernel(edge, open_ref, before_ref, behind_ref, coef_ref, c3_ref):
    cols = coef_ref.shape[1]
    lane = lax.broadcasted_iota(jnp.int32, (open_ref.shape[1], edge), 1)
    for c in range(open_ref.shape[0]):
        left = jnp.where(lane == 0, before_ref[c] * coef_ref[:, :edge], 0.0)
        right = jnp.where(lane == edge - 1, behind_ref[c] * coef_ref[:, cols - edge :], 0.0)
        c3_ref[c, :, :edge] = open_ref[c, :, :edge] + left
        c3_ref[c, :, edge:] = open_ref[c, :, edge:] + right


def blocks_kernel(plan, levels, inverse_ref, *out_refs):
    width = inverse_ref.shape[2]
    lane = lax.broadcasted_iota(jnp.int32, (levels, width), 1)
    for out_ref, (out, sources) in zip(out_refs, plan(lax.axis_index("rad"))):
        rows = inverse_ref[0, pl.ds(pl.multiple_of(out * levels, levels), levels), :]
        total = jnp.zeros_like(rows)
        for k, source in enumerate(sources):
            shift = lax.rem(k * levels - source * levels + width, width)
            here = (lane >= k * levels) & (lane < (k + 1) * levels)
            total = jnp.where(here, pltpu.roll(rows, shift, 1), total)
        out_ref[...] = total[:, : len(sources) * levels]


def finish_kernel(edge, counts, *refs):
    out_ref = refs[-1]
    for c in range(out_ref.shape[0]):
        at, sums = 0, []
        for count in counts:
            total = refs[at][c]
            for ref in refs[at + 1 : at + count]:
                total = total + ref[c]
            sums.append(total)
            at += count
        a1, b1, b2, a2 = sums
        out_ref[c, :, :edge] = a2[:, :edge]
        out_ref[c, :, edge : 3 * edge] = a1
        out_ref[c, :, 3 * edge : 5 * edge] = b1
        out_ref[c, :, 5 * edge : 7 * edge] = b2
        out_ref[c, :, 7 * edge :] = a2[:, edge:]


def product(matrix, stacked):
    return jnp.einsum("kl,cln->ckn", matrix, stacked, precision=lax.Precision.HIGH)


def body(adjoint_field, lateral_coef, radial_inverse, traction, face_plate, owned_plate):
    n_rad, n_lat = lax.axis_size("rad"), lax.axis_size("lat")
    lat = lax.axis_index("lat")
    comps, levels, cols = adjoint_field.shape
    near = max(d for d in range(1, n_rad + 1) if n_rad % d == 0 and d * d <= n_rad)
    far = n_rad // near
    edge = cols // 8

    def hop_rad(x, k, size, stride):
        return lax.ppermute(x, "rad", [(i, moved(i, k, size, stride)) for i in range(n_rad)])

    def plan(rad):
        def members(size, stride):
            at = lax.rem(lax.div(rad, stride), size)
            return [rad + (lax.rem(at + k, size) - at) * stride for k in range(size)]

        in_far, in_near = members(far, near), members(near, 1)
        return [(o, in_far) for o in in_near] + [(o, in_near) for o in in_far]

    def gather_a(x):
        return [x] + [hop_rad(x, -k, far, near) for k in range(1, far)]

    def gather_b(x):
        return [x] + [hop_rad(x, -k, near, 1) for k in range(1, near)]

    x, coef = adjoint_field, lateral_coef
    wide, thin = (comps, levels, 2 * edge), (comps, levels, 1)
    shapes = (wide, wide, wide, wide, thin, thin)
    a1, b1, b2, a2_open, first, last = vmem_call(lambda *refs: smooth_kernel(edge, *refs), shapes, x, coef, limit=None)
    blocks_a1, blocks_b1 = gather_a(a1), gather_b(b1)
    up = [(i, (i + 1) % n_lat) for i in range(n_lat)]
    before = lax.ppermute(last, "lat", up)
    behind = lax.ppermute(first, "lat", [(j, i) for i, j in up])
    (a2,) = vmem_call(lambda *refs: close_kernel(edge, *refs), (wide,), on_chip(a2_open), on_chip(before), on_chip(behind), coef)
    blocks_a2, blocks_b2 = gather_a(a2), gather_b(b2)

    plate_ids = face_plate[:, 0]
    matches = (plate_ids[:, None] == owned_plate[None, :]).astype(jnp.float32)
    sums = jnp.dot(matches.T, traction, precision=lax.Precision.HIGHEST)
    half, k = n_lat // 2, 0
    while half >= 1:
        bit = lat // half % 2
        keep = lax.dynamic_slice_in_dim(sums, bit * half, half, 0)
        send = lax.dynamic_slice_in_dim(sums, (1 - bit) * half, half, 0)
        sums = keep + lax.ppermute(send, "lat", [(i, i ^ half) for i in range(n_lat)])
        half //= 2
        k += 1
    total = sums
    for k in range(1, n_rad):
        total = total + lax.ppermute(sums, "rad", [(i, (i + k) % n_rad) for i in range(n_rad)])
    plate_grad = total * (1.0 / math.sqrt(traction.shape[0] * n_rad))

    shapes = [(levels, far * levels)] * near + [(levels, near * levels)] * far
    matrices = vmem_call(lambda *refs: blocks_kernel(plan, levels, *refs), shapes, radial_inverse)

    def columns(x, blocks, matrices, stride):
        stacked = jnp.concatenate(blocks, axis=1)
        size = len(matrices)
        sent = [product(m, stacked) for m in matrices[1:]]
        back = [hop_rad(p, k, size, stride) for k, p in enumerate(sent, 1)]
        own = lax.optimization_barrier(x + product(matrices[0], stacked))
        return [own, *back]

    for_a, for_b = matrices[:near], matrices[near:]
    parts = (
        columns(a1, blocks_a1, for_a, 1),
        columns(b1, blocks_b1, for_b, near),
        columns(b2, blocks_b2, for_b, near),
        columns(a2, blocks_a2, for_a, 1),
    )
    counts = [len(p) for p in parts]
    (corrected,) = vmem_call(
        lambda *refs: finish_kernel(edge, counts, *refs),
        (x.shape,),
        *[on_chip(p) for group in parts for p in group],
        space=jax.ShapeDtypeStruct,
    )
    return (corrected, plate_grad)


def solution(mesh):
    in_specs = (
        P(None, "rad", "lat"),
        P("rad", "lat"),
        P("lat", None, None),
        P(("lat", "rad"), None),
        P(("lat", "rad"), None),
        P(),
    )
    out_specs = (P(None, "rad", "lat"), P("lat", None))
    return jax.shard_map(body, mesh=mesh, in_specs=in_specs, out_specs=out_specs, check_vma=False)
```

```python
import math

import jax
import jax.numpy as jnp
from jax import lax
from jax.experimental import pallas as pl
from jax.experimental.pallas import tpu as pltpu
from jax.sharding import PartitionSpec as P

VMEM_BYTES = 8 << 20


def moved(i, k, size, stride):
    at = i // stride % size
    return i + ((at + k) % size - at) * stride


def on_chip(x):
    return pltpu.with_memory_space_constraint(x, pltpu.VMEM)


def vmem_call(kernel, out_shapes, *args, space=pltpu.VMEM, limit=VMEM_BYTES):
    return pl.pallas_call(
        kernel,
        out_shape=[space(s, jnp.float32) for s in out_shapes],
        in_specs=[pl.BlockSpec(memory_space=pltpu.VMEM)] * len(args),
        out_specs=[pl.BlockSpec(memory_space=pltpu.VMEM)] * len(out_shapes),
        compiler_params=pltpu.CompilerParams(vmem_limit_bytes=limit),
    )(*args)


def smooth_kernel(edge, x_ref, coef_ref, a1_ref, b1_ref, b2_ref, a2_ref, first_ref, last_ref):
    comps, _, cols = x_ref.shape
    lane = lax.broadcasted_iota(jnp.int32, x_ref.shape[1:], 1)
    coef = coef_ref[...]
    for c in range(comps):
        x = x_ref[c]
        before = jnp.where(lane == 0, 0.0, pltpu.roll(x, 1, 1))
        behind = jnp.where(lane == cols - 1, 0.0, pltpu.roll(x, cols - 1, 1))
        smooth = x + coef * (before + behind - 2.0 * x)
        a1_ref[c] = smooth[:, edge : 3 * edge]
        b1_ref[c] = smooth[:, 3 * edge : 5 * edge]
        b2_ref[c] = smooth[:, 5 * edge : 7 * edge]
        a2_ref[c, :, :edge] = smooth[:, :edge]
        a2_ref[c, :, edge:] = smooth[:, 7 * edge :]
        first_ref[c : c + 1] = x[:, :edge].T[:1]
        last_ref[c : c + 1] = x[:, cols - edge :].T[edge - 1 :]


def close_kernel(edge, open_ref, before_ref, behind_ref, coef_ref, a2_ref):
    cols = coef_ref.shape[1]
    lane = lax.broadcasted_iota(jnp.int32, (open_ref.shape[1], edge), 1)
    before, behind = before_ref[...].T, behind_ref[...].T
    for c in range(open_ref.shape[0]):
        left = jnp.where(lane == 0, before[:, c : c + 1] * coef_ref[:, :edge], 0.0)
        right = jnp.where(lane == edge - 1, behind[:, c : c + 1] * coef_ref[:, cols - edge :], 0.0)
        a2_ref[c, :, :edge] = open_ref[c, :, :edge] + left
        a2_ref[c, :, edge:] = open_ref[c, :, edge:] + right


def blocks_kernel(plan, levels, inverse_ref, *out_refs):
    width = inverse_ref.shape[2]
    lane = lax.broadcasted_iota(jnp.int32, (levels, width), 1)
    for out_ref, (out, sources) in zip(out_refs, plan(lax.axis_index("rad"))):
        rows = inverse_ref[0, pl.ds(pl.multiple_of(out * levels, levels), levels), :]
        total = jnp.zeros_like(rows)
        for k, source in enumerate(sources):
            shift = lax.rem(k * levels - source * levels + width, width)
            here = (lane >= k * levels) & (lane < (k + 1) * levels)
            total = jnp.where(here, pltpu.roll(rows, shift, 1), total)
        out_ref[...] = total[:, : len(sources) * levels]


def finish_kernel(edge, counts, scale, n_plates, *refs):
    plates, parts = refs[:n_plates], refs[n_plates:-2]
    out_ref, grad_ref = refs[-2:]
    total = plates[0][...]
    for ref in plates[1:]:
        total = total + ref[...]
    grad_ref[...] = total * scale
    for c in range(out_ref.shape[0]):
        at, sums = 0, []
        for count in counts:
            total = parts[at][c]
            for ref in parts[at + 1 : at + count]:
                total = total + ref[c]
            sums.append(total)
            at += count
        a1, b1, b2, a2 = sums
        out_ref[c, :, :edge] = a2[:, :edge]
        out_ref[c, :, edge : 3 * edge] = a1
        out_ref[c, :, 3 * edge : 5 * edge] = b1
        out_ref[c, :, 5 * edge : 7 * edge] = b2
        out_ref[c, :, 7 * edge :] = a2[:, edge:]


def product(matrix, stacked):
    return jnp.einsum("kl,cln->ckn", matrix, stacked, precision=lax.Precision.HIGH)


def body(adjoint_field, lateral_coef, radial_inverse, traction, face_plate, owned_plate):
    n_rad, n_lat = lax.axis_size("rad"), lax.axis_size("lat")
    lat = lax.axis_index("lat")
    comps, levels, cols = adjoint_field.shape
    near = max(d for d in range(1, n_rad + 1) if n_rad % d == 0 and d * d <= n_rad)
    far = n_rad // near
    edge = cols // 8

    def hop_rad(x, k, size, stride):
        return lax.ppermute(x, "rad", [(i, moved(i, k, size, stride)) for i in range(n_rad)])

    def plan(rad):
        def members(size, stride):
            at = lax.rem(lax.div(rad, stride), size)
            return [rad + (lax.rem(at + k, size) - at) * stride for k in range(size)]

        in_far, in_near = members(far, near), members(near, 1)
        return [(o, in_far) for o in in_near] + [(o, in_near) for o in in_far]

    def gather_a(x):
        return [x] + [hop_rad(x, -k, far, near) for k in range(1, far)]

    def gather_b(x):
        return [x] + [hop_rad(x, -k, near, 1) for k in range(1, near)]

    x, coef = adjoint_field, lateral_coef
    wide, thin = (comps, levels, 2 * edge), (comps, levels)
    shapes = (wide, wide, wide, wide, thin, thin)
    a1, b1, b2, a2_open, first, last = vmem_call(lambda *refs: smooth_kernel(edge, *refs), shapes, x, coef, limit=None)
    blocks_a1, blocks_b1 = gather_a(a1), gather_b(b1)
    up = [(i, (i + 1) % n_lat) for i in range(n_lat)]
    before = lax.ppermute(last, "lat", up)
    behind = lax.ppermute(first, "lat", [(j, i) for i, j in up])
    (a2,) = vmem_call(lambda *refs: close_kernel(edge, *refs), (wide,), on_chip(a2_open), on_chip(before), on_chip(behind), coef)
    blocks_a2, blocks_b2 = gather_a(a2), gather_b(b2)

    plate_ids = face_plate[:, 0]
    matches = (plate_ids[:, None] == owned_plate[None, :]).astype(jnp.float32)
    sums = jnp.dot(matches.T, traction, precision=lax.Precision.HIGHEST)
    half, k = n_lat // 2, 0
    while half >= 1:
        bit = lat // half % 2
        keep = lax.dynamic_slice_in_dim(sums, bit * half, half, 0)
        send = lax.dynamic_slice_in_dim(sums, (1 - bit) * half, half, 0)
        sums = keep + lax.ppermute(send, "lat", [(i, i ^ half) for i in range(n_lat)])
        half //= 2
        k += 1
    plates = [sums]
    for k in range(1, n_rad):
        plates.append(lax.ppermute(sums, "rad", [(i, (i + k) % n_rad) for i in range(n_rad)]))
    scale = 1.0 / math.sqrt(traction.shape[0] * n_rad)

    shapes = [(levels, far * levels)] * near + [(levels, near * levels)] * far
    matrices = vmem_call(lambda *refs: blocks_kernel(plan, levels, *refs), shapes, radial_inverse)

    def columns(x, blocks, matrices, stride):
        stacked = jnp.concatenate(blocks, axis=1)
        size = len(matrices)
        sent = [product(m, stacked) for m in matrices[1:]]
        back = [hop_rad(p, k, size, stride) for k, p in enumerate(sent, 1)]
        own = lax.optimization_barrier(x + product(matrices[0], stacked))
        return [own, *back]

    for_a, for_b = matrices[:near], matrices[near:]
    parts = (
        columns(a1, blocks_a1, for_a, 1),
        columns(b1, blocks_b1, for_b, near),
        columns(b2, blocks_b2, for_b, near),
        columns(a2, blocks_a2, for_a, 1),
    )
    counts = [len(p) for p in parts]
    corrected, plate_grad = vmem_call(
        lambda *refs: finish_kernel(edge, counts, scale, n_rad, *refs),
        (x.shape, sums.shape),
        *[on_chip(p) for p in plates],
        *[on_chip(p) for group in parts for p in group],
        space=jax.ShapeDtypeStruct,
    )
    return (corrected, plate_grad)


def solution(mesh):
    in_specs = (
        P(None, "rad", "lat"),
        P("rad", "lat"),
        P("lat", None, None),
        P(("lat", "rad"), None),
        P(("lat", "rad"), None),
        P(),
    )
    out_specs = (P(None, "rad", "lat"), P("lat", None))
    return jax.shard_map(body, mesh=mesh, in_specs=in_specs, out_specs=out_specs, check_vma=False)
```
